128 devices in a mesh: tm: 8 (over y_lo, x), chan: 16 (over z, y_hi, core).
Axes of the slice: x: 4, y: 4 (y_hi: 2, y_lo: 2; y = y_hi * 2 + y_lo), z: 4, core: 2. Of those that a mesh axis runs over, the one named last changes fastest.
Arguments:
- samples: bfloat16 [1024, 262144], P('tm', 'chan'), may hold values from -6 to 6
- valid: int32 [1024, 32], P('tm', 'chan'), may hold values from 0 to 1, as said below
Outputs:
- average: float32 [1024, 4224], P(('tm', 'chan'))
The draws below stay inside these ranges and needn't reach their ends.
Inputs may be any that keep to these rules, and one draw needn't show every extreme that they name: `valid`: split the channels into aligned groups of 128; in every segment each group has at most 96 entries equal to 1, and exactly 96 for some group and segment; at least one channel has no 1 in any segment.
All inputs are finite; a program needn't handle non-finite values.
Results may differ from the reference program's by a relative error of at most 0.0026.
Values may be sent and summed in bfloat16 or wider, within the bound.
A program may use at most 128 MiB of HBM per device.

```python
import jax
import jax.numpy as jnp
from jax import lax

CHANNELS = 1024
RADIX = 128
KBANDS = 33
SEGMENTS = 32
TIME = 262144
MOSTV = 96
N_TM = 8


def draw_samples(key, part):
    streams = jax.random.split(jax.random.fold_in(key, 17), 3)
    offset = jax.random.uniform(streams[0], (CHANNELS, 1), jnp.float32, -1.5, 1.5)
    values = offset + jax.random.normal(streams[2], (CHANNELS, TIME), jnp.float32)
    return jnp.clip(values, -6.0, 6.0).astype(jnp.bfloat16)


def draw_valid(key, part):
    keys = jax.random.split(key, 5)
    cluster_size_number = CHANNELS // N_TM
    cell_index = jnp.arange(N_TM * SEGMENTS, dtype=jnp.int32).reshape(N_TM, SEGMENTS)
    channel_index = jnp.arange(CHANNELS, dtype=jnp.int32)
    per_cell = jax.random.randint(keys[0], (N_TM, SEGMENTS), cluster_size_number // 8, MOSTV + 1)
    fullest = jax.random.randint(keys[1], (), 0, N_TM * SEGMENTS)
    per_cell = jnp.where(cell_index == fullest, MOSTV, per_cell)
    missing_jitter_term = jax.random.randint(keys[2], (CHANNELS,), 0, 32) == 0
    dead_forced = channel_index == jax.random.randint(keys[3], (), 0, CHANNELS)
    priority_levels = jax.random.randint(keys[4], (N_TM, SEGMENTS, cluster_size_number), 0, 1 << 16)
    missing_reward = jnp.where(missing_jitter_term, 1 << 16, 0).reshape(N_TM, 1, cluster_size_number)
    priority_levels = priority_levels + missing_reward
    priority_levels = jnp.where(dead_forced.reshape(N_TM, 1, cluster_size_number), 1 << 17, priority_levels)
    inside = jnp.arange(cluster_size_number, dtype=jnp.int32)
    distinct = priority_levels * cluster_size_number + inside[None, None, :]
    order = jnp.argsort(distinct, axis=2)
    ranking = jnp.argsort(order, axis=2)
    chosen = (ranking < per_cell[:, :, None]).astype(jnp.int32)
    return jnp.transpose(chosen, (0, 2, 1)).reshape(CHANNELS, SEGMENTS)


def setup_inputs(seed: int = 0) -> dict:
    arg_keys = jax.random.split(jax.random.key(seed), 3)
    samples = draw_samples(jax.random.fold_in(arg_keys[2], 71), 0)
    valid = draw_valid(jax.random.fold_in(arg_keys[2], 71), 0)
    return {"samples": samples, "valid": valid}


full_turn = 6.283185307179586


def make_tables():
    seg_len = RADIX * RADIX
    counter = jnp.arange(RADIX, dtype=jnp.int32)
    inner_prod = (counter[:, None] * counter[None, :]) % RADIX
    angle_one = full_turn * inner_prod.astype(jnp.float32) / RADIX
    cos_one = jnp.cos(angle_one).astype(jnp.bfloat16)
    sin_one = jnp.sin(angle_one).astype(jnp.bfloat16)
    outer_prod = (counter[:, None] * counter[None, :]) % seg_len
    angle_mid = full_turn * outer_prod.astype(jnp.float32) / seg_len
    twid_real = jnp.cos(angle_mid)
    twid_imag = -jnp.sin(angle_mid)
    band_index = jnp.arange(KBANDS, dtype=jnp.int32)
    angle_two = full_turn * ((counter[:, None] * band_index[None, :]) % RADIX).astype(jnp.float32) / RADIX
    cos_two = jnp.cos(angle_two).astype(jnp.bfloat16)
    sine_double_angle = jnp.sin(angle_two).astype(jnp.bfloat16)
    places = jnp.arange(seg_len, dtype=jnp.int32).astype(jnp.float32)
    window = 0.5 - 0.5 * jnp.cos(full_turn * places / seg_len)
    weight_sum = jnp.sum(window * window)
    onesided = jnp.where(jnp.arange(KBANDS * RADIX, dtype=jnp.int32) == 0, 1.0, 2.0).astype(jnp.float32) / weight_sum
    return (cos_one, sin_one, twid_real, twid_imag, cos_two, sine_double_angle, window, onesided)


def contract(left, right, form):
    return jnp.einsum(form, left.astype(jnp.float32), right.astype(jnp.float32))


def spectrum(segment, tables):
    cos_one, sin_one, twid_real, twid_imag, cos_two, sine_double_angle, window, onesided = tables
    height = segment.shape[0]
    values = segment.astype(jnp.float32)
    centred = values - jnp.mean(values, axis=1, keepdims=True)
    shaped = (centred * window[None, :]).astype(jnp.bfloat16).reshape(height, RADIX, RADIX)
    first_real = contract(shaped, cos_one, "cnm,nk->ckm")
    first_imag = -contract(shaped, sin_one, "cnm,nk->ckm")
    mid_real = (first_real * twid_real - first_imag * twid_imag).astype(jnp.bfloat16)
    mid_imag = (first_real * twid_imag + first_imag * twid_real).astype(jnp.bfloat16)
    last_real = contract(mid_real, cos_two, "ckn,nm->cmk") + contract(mid_imag, sine_double_angle, "ckn,nm->cmk")
    closing_quadrature_part = contract(mid_imag, cos_two, "ckn,nm->cmk") - contract(mid_real, sine_double_angle, "ckn,nm->cmk")
    return (last_real * last_real + closing_quadrature_part * closing_quadrature_part).reshape(height, -1) * onesided[None, :]


def block_power(segments, tables):
    height = segments.shape[0]
    block_rows = 128 if height % 128 == 0 else height

    def one_block(piece):
        return spectrum(piece, tables)

    final_output = lax.map(one_block, segments.reshape(height // block_rows, block_rows, -1))
    return final_output.reshape(height, -1)


def reference(samples, valid):
    tables = make_tables()
    seg_len = RADIX * RADIX
    half_len = seg_len // 2
    padded = jnp.concatenate([samples, jnp.zeros((CHANNELS, half_len), jnp.bfloat16)], axis=1)

    def accumulate(cumulative_tally, segment_index):
        start = (segment_index * half_len).astype(jnp.int32)
        segment = lax.dynamic_slice_in_dim(padded, start, seg_len, 1)
        powers = block_power(segment, tables)
        weights = lax.dynamic_slice_in_dim(valid, segment_index, 1, 1).astype(jnp.float32)
        return cumulative_tally + weights * powers, None

    initial = jnp.zeros((CHANNELS, KBANDS * RADIX), jnp.float32)
    totals, _ = lax.scan(accumulate, initial, jnp.arange(SEGMENTS, dtype=jnp.int32))
    tallied_count = jnp.sum(valid, axis=1).astype(jnp.float32)
    return totals / jnp.maximum(tallied_count, 1.0)[:, None]
```

```python
import jax
import jax.numpy as jnp
import numpy as np
from jax import lax
from jax.experimental import pallas as pl
from jax.experimental.pallas import tpu as pltpu
from jax.sharding import PartitionSpec as P

RADIX = 128
KBANDS = 33
SEG = RADIX * RADIX
HALF = SEG // 2
CHIPS = 8
ROWS = 40
MESH = pl.DeviceIdType.MESH
f32, bf16 = jnp.float32, jnp.bfloat16


def make_tables():
    a, k, m = np.arange(RADIX), np.arange(RADIX // 2), np.arange(RADIX)
    turn = 2 * np.pi
    inner = turn * ((k[:, None] * a[None, :]) % RADIX) / RADIX
    dft_in = np.concatenate([np.cos(inner), -np.sin(inner)])
    dft_in[RADIX // 2] = np.cos(np.pi * a)
    angle = turn * (k[:, None] * m[None, :]) / SEG
    real, imag = np.cos(angle), -np.sin(angle)
    real_b = real.copy()
    real_b[0] = 0
    mirror = turn * (((RADIX - k)[:, None] * m[None, :]) % SEG) / SEG
    m_real, m_imag = np.cos(mirror), -np.sin(mirror)
    angle_64 = turn * (RADIX // 2) * m / SEG
    p1, p2, p3, p4 = m_real.copy(), m_imag.copy(), m_imag.copy(), m_real.copy()
    p1[0], p2[0], p3[0], p4[0] = 0, np.cos(angle_64), 0, np.sin(angle_64)
    twiddle = np.stack([real, imag, real_b, p1, p2, p3, p4])
    j = np.arange(KBANDS)
    outer = turn * ((j[:, None] * m[None, :]) % RADIX) / RADIX
    cos, sin = np.cos(outer), np.sin(outer)
    dft_out = np.zeros((2 * ROWS, 2 * RADIX))
    dft_out[:KBANDS, :RADIX], dft_out[:KBANDS, RADIX:] = cos, sin
    dft_out[ROWS : ROWS + KBANDS, :RADIX], dft_out[ROWS : ROWS + KBANDS, RADIX:] = -sin, cos
    window = (0.5 - 0.5 * np.cos(turn * np.arange(SEG) / SEG)).reshape(RADIX, RADIX)
    norm = float(np.sum(window * window))
    single = lambda t: np.asarray(t, np.float32)
    return (
        single(dft_in).astype(jnp.bfloat16),
        single(dft_out).astype(jnp.bfloat16),
        single(twiddle),
        single(window),
        norm,
    )


def kernel(
    norm, x_ref, valid_ref, dft_in, dft_out, tw, win, out_ref,
    buf, halo, vloc, vpair, vhalo, vf, blocks, sums, tot, snd, rcv, fin,
    own_sem, pair_send, pair_recv, halo_send, halo_recv,
    v_send, v_recv, part_send, part_recv,
):
    me = lax.axis_index("chan")
    chip, core = me // 2, me % 2
    nxt, prv = (chip + 1) % CHIPS, (chip + CHIPS - 1) % CHIPS

    def chan(c, h):
        return {"chan": c * 2 + h}

    def slab_of(c, p):
        return (c + 2 * p + 1 - 7 * (p // 4)) % CHIPS

    def rows(g, h):
        return pl.ds(pl.multiple_of(g * 16 + h * 8, 8), 8)

    def own_copy(g):
        return pltpu.make_async_copy(x_ref.at[rows(g, core)], buf.at[core, g], own_sem.at[g])

    def remote(src, dst, send, recv, where):
        return pltpu.make_async_remote_copy(
            src_ref=src, dst_ref=dst, send_sem=send, recv_sem=recv,
            device_id=where, device_id_type=MESH,
        )

    def pair_copy(g, slot):
        return remote(
            x_ref.at[rows(g, 1 - core)], buf.at[slot, g],
            pair_send.at[g], pair_recv.at[g], chan(chip, 1 - core),
        )

    def halo_copy(g, h):
        return remote(
            x_ref.at[rows(g, h), pl.ds(HALF, HALF)], halo.at[g],
            halo_send.at[g, h], halo_recv.at[g], chan(nxt, h),
        )

    def part_copy(g, slot):
        return remote(snd.at[g], rcv.at[slot], part_send.at[g], part_recv.at[slot], chan(g, core))

    barrier = pltpu.get_barrier_semaphore()
    pl.semaphore_signal(barrier, 1, device_id=chan(chip, 1 - core), device_id_type=MESH)
    for d in range(1, CHIPS):
        pl.semaphore_signal(barrier, 1, device_id=chan((chip + d) % CHIPS, core), device_id_type=MESH)

    @pl.when(core == 0)
    def _():
        pl.semaphore_signal(barrier, 1, device_id=chan(prv, 1), device_id_type=MESH)

    def start_own(p, c):
        own_copy(slab_of(chip, p)).start()
        return c

    lax.fori_loop(0, CHIPS, start_own, 0)
    seen = valid_ref[...].astype(f32)
    for t in range(2):
        wide = jnp.broadcast_to(seen[:, t : t + 1], (RADIX, RADIX)).reshape(CHIPS, 2, 8, RADIX)
        for h in range(2):
            vloc[t, h] = wide[:, h].reshape(64, RADIX).astype(bf16)
    pl.semaphore_wait(barrier, CHIPS + core)

    v_pair = [
        remote(vloc.at[t, 1 - core], vpair.at[t], v_send.at[t], v_recv.at[t], chan(chip, 1 - core))
        for t in range(2)
    ]
    v_halo = [remote(vloc.at[1, h], vhalo, v_send.at[2 + h], v_recv.at[2], chan(nxt, h)) for h in range(2)]

    def start_copies(p, c):
        pair_copy(slab_of(chip, p), core).start()

        @pl.when(core == 1)
        def _():
            for h in range(2):
                halo_copy(slab_of(nxt, p), h).start()

        return c

    for copy in v_pair:
        copy.start()

    @pl.when(core == 1)
    def _():
        for copy in v_halo:
            copy.start()

    lax.fori_loop(0, CHIPS, start_copies, 0)

    def unpack(b, g, src, lanes):
        acc = jnp.zeros((8, RADIX), f32)
        for a in range(64):
            piece = src[:, lanes + a * RADIX : lanes + (a + 1) * RADIX].astype(f32)
            blocks[b, g, a * 8 : (a + 1) * 8, :] = piece
            acc = acc + piece
        sums[b, g] = jnp.broadcast_to(jnp.sum(acc, axis=1, keepdims=True), (8, RADIX))

    def segment(t, g):
        mean = (sums[t, g] + sums[t + 1, g]) * (1.0 / SEG)
        weight = vf[t, pl.ds(pl.multiple_of(g * 8, 8), 8), :]
        for c2 in range(4):
            shaped = []
            for c in (2 * c2, 2 * c2 + 1):
                mu = mean[c : c + 1, :]
                lead = (blocks[t, g, pl.ds(c, 64, stride=8), :] - mu) * win[0:64, :]
                trail = (blocks[t + 1, g, pl.ds(c, 64, stride=8), :] - mu) * win[64:128, :]
                shaped.append(jnp.concatenate([lead.astype(bf16), trail.astype(bf16)], axis=0))
            first = jnp.dot(dft_in[...], jnp.concatenate(shaped, axis=1), preferred_element_type=f32)
            middle = []
            for h in range(2):
                re = first[0:64, h * RADIX : (h + 1) * RADIX]
                im = first[64:128, h * RADIX : (h + 1) * RADIX]
                low = [re * tw[0] - im * tw[1], re * tw[1] + im * tw[2]]
                high = [re * tw[3] + im * tw[4], re * tw[5] - im * tw[6]]
                for pair in (low, high):
                    middle.append(jnp.concatenate([part.astype(bf16) for part in pair], axis=1))
            last = lax.dot_general(
                dft_out[...], jnp.concatenate(middle, axis=0),
                (((1,), (1,)), ((), ())), preferred_element_type=f32,
            )
            re, im = last[0:ROWS], last[ROWS : 2 * ROWS]
            scale = jnp.concatenate([weight[2 * c2 : 2 * c2 + 1], weight[2 * c2 + 1 : 2 * c2 + 2]], axis=1)
            tot[g, :, c2 * 256 : (c2 + 1) * 256] += (re * re + im * im) * scale

    for copy in v_pair:
        copy.wait_recv()
    mine = [vloc[t, core].astype(f32) for t in range(2)]
    other = [vpair[t].astype(f32) for t in range(2)]
    first_core = core == 0
    vf[1] = jnp.where(first_core, mine[0], other[0])
    vf[2] = jnp.where(first_core, mine[1], other[1])
    vf[3] = jnp.where(first_core, other[0], mine[0])

    def local(p, c):
        g = slab_of(chip, p)
        own_copy(g).wait()
        pair_copy(g, 1 - core).wait_recv()
        for b in range(4):
            unpack(b + 1, g, buf.at[b // 2, g], (b % 2) * HALF)
        tot[g] = jnp.zeros((ROWS, 1024), f32)

        def one(t, c):
            segment(t, g)
            return c

        return lax.fori_loop(1, 4, one, c)

    lax.fori_loop(0, CHIPS, local, 0)

    @pl.when(chip == 0)
    def _():
        def clear(g, c):
            blocks[1, g] = jnp.zeros((512, RADIX), f32)
            sums[1, g] = jnp.zeros((8, RADIX), f32)
            return c

        lax.fori_loop(0, CHIPS, clear, 0)

    v_halo[0].wait_recv()
    vf[0] = vhalo[...].astype(f32)

    def arrived(p, c):
        g = slab_of(chip, p)
        halo_copy(g, 0).wait_recv()
        unpack(0, g, halo.at[g], 0)
        segment(0, g)
        at = pl.ds(pl.multiple_of(g * 8, 8), 8)
        count = vf[0, at, :] + vf[1, at, :] + vf[2, at, :] + vf[3, at, :]
        tot[g, 33:34, :] = jnp.concatenate([count[c : c + 1] for c in range(8)], axis=1)
        snd[g] = tot[g].astype(bf16)

        @pl.when(p < CHIPS - 1)
        def _():
            part_copy(g, chip).start()

        return c

    lax.fori_loop(0, CHIPS, arrived, 0)

    fin[...] = tot[chip]

    def gather(p, c):
        s = slab_of(chip, p)
        part_copy(s, s).wait_recv()
        fin[...] += rcv[s].astype(f32)
        return c

    lax.fori_loop(0, CHIPS - 1, gather, 0)
    lane = lax.broadcasted_iota(jnp.int32, (ROWS, RADIX), 1)
    row = lax.broadcasted_iota(jnp.int32, (ROWS, RADIX), 0)
    scale = jnp.where((lane == 0) & (row == 0), 1.0, 2.0) * (1.0 / norm)
    order = jnp.where(lane <= 64, lane, 192 - lane)
    for c in range(8):
        power = fin[:, c * RADIX : (c + 1) * RADIX]
        average = power * scale / jnp.maximum(power[33:34, :], 1.0)
        average = jnp.take_along_axis(average, order, axis=1)
        sums_out = blocks.at[0, 0]
        sums_out[pl.ds(c, KBANDS, stride=8), :] = average[0:KBANDS]
    for j in range(KBANDS):
        out_ref[:, j * RADIX : (j + 1) * RADIX] = blocks[0, 0, j * 8 : (j + 1) * 8, :]

    def drain(p, c):
        g = slab_of(chip, p)
        pair_copy(g, core).wait_send()

        @pl.when(p < CHIPS - 1)
        def _():
            part_copy(g, chip).wait_send()

        @pl.when(core == 1)
        def _():
            for h in range(2):
                halo_copy(g, h).wait_send()

        return c

    lax.fori_loop(0, CHIPS, drain, 0)
    for copy in v_pair:
        copy.wait_send()

    @pl.when(core == 1)
    def _():
        for copy in v_halo:
            copy.wait_send()


def per_device(samples, valid):
    dft_in, dft_out, twiddle, window, norm = make_tables()
    vmem = pl.BlockSpec(memory_space=pltpu.VMEM)
    dma = pltpu.SemaphoreType.DMA
    return pl.pallas_call(
        lambda *refs: kernel(norm, *refs),
        out_shape=jax.ShapeDtypeStruct((8, KBANDS * RADIX), f32),
        in_specs=[pl.BlockSpec(memory_space=pl.ANY)] + [vmem] * 5,
        out_specs=vmem,
        scratch_shapes=[
            pltpu.VMEM((2, CHIPS, 8, SEG), bf16),
            pltpu.VMEM((CHIPS, 8, HALF), bf16),
            pltpu.VMEM((2, 2, 64, RADIX), bf16),
            pltpu.VMEM((2, 64, RADIX), bf16),
            pltpu.VMEM((64, RADIX), bf16),
            pltpu.VMEM((4, 64, RADIX), f32),
            pltpu.VMEM((5, CHIPS, 512, RADIX), f32),
            pltpu.VMEM((5, CHIPS, 8, RADIX), f32),
            pltpu.VMEM((CHIPS, ROWS, 1024), f32),
            pltpu.VMEM((CHIPS, ROWS, 1024), bf16),
            pltpu.VMEM((CHIPS, ROWS, 1024), bf16),
            pltpu.VMEM((ROWS, 1024), f32),
            dma((CHIPS,)), dma((CHIPS,)), dma((CHIPS,)), dma((CHIPS, 2)), dma((CHIPS,)),
            dma((4,)), dma((3,)), dma((CHIPS,)), dma((CHIPS,)),
        ],
        compiler_params=pltpu.CompilerParams(
            collective_id=0, has_side_effects=True, vmem_limit_bytes=56 * 2**20
        ),
    )(samples, valid, dft_in, dft_out, twiddle, window)


def solution(mesh):
    return jax.shard_map(
        per_device,
        mesh=mesh,
        in_specs=(P("tm", "chan"), P("tm", "chan")),
        out_specs=P(("tm", "chan"), None),
        check_vma=False,
    )
```
